32 devices in a mesh: dp: 2 (over x), seq: 16 (over z, y, core).
Axes of the slice: x: 2, y: 2, z: 4, core: 2. Of those that a mesh axis runs over, the one named last changes fastest.
Arguments:
- queries: bfloat16 [4096, 1024], P(('dp', 'seq')), parts along dimension 0, may hold values from -6 to 6
- keys: bfloat16 [4096, 1024], P(('dp', 'seq')), parts along dimension 0, may hold values from -6 to 6
- values: bfloat16 [4096, 1024], P(('dp', 'seq')), parts along dimension 0, may hold values from -36 to 36
- feat_weight: bfloat16 [16, 64, 256], replicated, may hold values from -0.75 to 0.75
- norm_gain: bfloat16 [1024], replicated, may hold values from 0.25 to 1.75
- counts: int32 [32, 16], P('dp'), parts along dimension 0, may hold values from 4 to 12, as said below
- offsets: int32 [32, 16], P('dp'), parts along dimension 0, may hold values from 0 to 127, as said below
Outputs:
- mixed: bfloat16 [4096, 1024], P(('dp', 'seq')), parts along dimension 0
The draws below stay inside these ranges and needn't reach their ends.
There are 2 independent parts, one for each index of `dp`. The reference program is written for one: setup_inputs(seed, part) draws one part's arguments, and reference() takes and returns one part's arrays. A program takes and returns all parts, laid end to end along the dimension named above; an argument that names none is the same for every part. Nothing has to cross between parts.
Inputs may be any that keep to these rules, and one draw needn't show every extreme that they name: Each row and each column of counts sums to 128; every loader sends 12 rows to exactly one device. For each device d the ranges from offsets[j, d] to offsets[j, d] + counts[j, d] - 1 over all loaders j tile 0 to 127.
All inputs are finite; a program needn't handle non-finite values.
Results may differ from the reference program's by a relative error of at most 0.0023.
Values may be sent and summed in bfloat16 or wider, within the bound.
A program may use at most 192 MiB of HBM per device.

```python
import jax
import jax.numpy as jnp
from jax import lax

HEADS = 16
HEAD = 64
FEAT = 256
VDIM = 64
TOK_DEV = 128
TOKENS = 2048
BASE = 8
SPREAD = 4
N_SEQ = 16


def route_tables(key):
    table_key = jax.random.fold_in(key, 7)
    first_key, second_key, third_key = jax.random.split(table_key, 3)
    sigma = jax.random.permutation(first_key, N_SEQ).astype(jnp.int32)
    shifts = jax.random.randint(second_key, (SPREAD,), 1, N_SEQ).astype(jnp.int32)
    loaders = jnp.arange(N_SEQ, dtype=jnp.int32)
    peak = (loaders[None, :] == sigma[:, None]).astype(jnp.int32)
    taken_index = sigma[(loaders[None, :] + shifts[:, None]) % N_SEQ]
    taken = jnp.sum((taken_index[:, :, None] == loaders[None, None, :]).astype(jnp.int32), axis=0)
    counts = (BASE + SPREAD * peak - taken).astype(jnp.int32)
    order_keys = jax.random.split(third_key, N_SEQ)
    ranks = jax.vmap(lambda one_key: jax.random.permutation(one_key, N_SEQ))(order_keys).T.astype(jnp.int32)
    before = (ranks[None, :, :] < ranks[:, None, :]).astype(jnp.int32)
    offsets = jnp.sum(before * counts[None, :, :], axis=1).astype(jnp.int32)
    return (counts, offsets)


def draw_counts(key, part):
    return route_tables(key)[0]


def draw_offsets(key, part):
    return route_tables(key)[1]


def draw_values(key, part):
    value_key = jax.random.fold_in(key, 11)
    base_key, row_key, column_key = jax.random.split(value_key, 3)
    row_scale = jnp.exp(jax.random.uniform(row_key, (TOKENS, 1), jnp.float32, jnp.log(0.3), jnp.log(3.0)))
    column_scale = jnp.exp(jax.random.uniform(column_key, (1, HEADS * VDIM), jnp.float32, jnp.log(0.3), jnp.log(3.0)))
    basic = jnp.clip(jax.random.normal(base_key, (TOKENS, HEADS * VDIM), jnp.float32), -4.0, 4.0)
    return (basic * row_scale * column_scale).astype(jnp.bfloat16)


def steps_of(key, dims, cuts, least, largest):
    loudness = 1.0
    for dim, shards_of in cuts:
        draws = jax.random.uniform(jax.random.fold_in(jax.random.fold_in(key, 6), dim), (shards_of,), jnp.float32, least / len(cuts), largest / len(cuts))
        loudness = loudness * jnp.repeat(jnp.exp(draws), dims[dim] // shards_of).reshape((-1,) + (1,) * (len(dims) - 1 - dim))
    return loudness


def normal_values(stream_key, dims, spread, most, cuts=(), kind=jnp.bfloat16):
    level = steps_of(stream_key, dims, cuts, -0.22, 0.18) if cuts else 1.0
    entries = jax.random.normal(stream_key, dims, jnp.float32) * spread * level
    return jnp.minimum(jnp.maximum(entries, -most), most).astype(kind)


def setup_inputs(seed: int = 0, part: int = 0) -> dict:
    key_of = jax.random.split(jax.random.key(seed), 8)
    part_keys = jax.random.split(jax.random.fold_in(key_of[7], part), 8)
    queries = normal_values(part_keys[0], (TOKENS, HEADS * HEAD), 1.0, 6.0, ((0, 16),))
    keys = normal_values(part_keys[1], (TOKENS, HEADS * HEAD), 1.0, 6.0, ((0, 16),))
    values = draw_values(jax.random.fold_in(jax.random.fold_in(key_of[7], part), 71), part)
    feat_weight = normal_values(key_of[3], (HEADS, HEAD, FEAT), HEAD ** -0.5, 0.75)
    norm_gain = jnp.clip(1.0 + 0.15 * jax.random.normal(key_of[4], (HEADS * VDIM,), jnp.float32), 0.25, 1.75).astype(jnp.bfloat16)
    counts = draw_counts(jax.random.fold_in(jax.random.fold_in(key_of[7], part), 71), part)
    offsets = draw_offsets(jax.random.fold_in(jax.random.fold_in(key_of[7], part), 71), part)
    return {"queries": queries, "keys": keys, "values": values, "feat_weight": feat_weight, "norm_gain": norm_gain, "counts": counts, "offsets": offsets}


def trace_positions(counts, offsets):
    starts = (jnp.cumsum(counts, axis=1) - counts).astype(jnp.int32)
    inner = jnp.arange(TOK_DEV, dtype=jnp.int32)
    device_ids = jnp.arange(N_SEQ, dtype=jnp.int32)

    def one_loader(start_row, count_row, offset_row):
        inside = (inner[:, None] >= start_row[None, :]) & (inner[:, None] < (start_row + count_row)[None, :])
        hot = inside.astype(jnp.int32)
        target = lax.optimization_barrier(jnp.sum(hot * device_ids[None, :], axis=1)).astype(jnp.int32)
        shift = lax.optimization_barrier(jnp.sum(hot * (offset_row - start_row)[None, :], axis=1)).astype(jnp.int32)
        return (target * TOK_DEV + shift + inner).astype(jnp.int32)
    return jax.vmap(one_loader)(starts, counts, offsets).reshape(-1)

def feature_map(rows, feat_weight):
    split_rows = rows.reshape(rows.shape[0], HEADS, HEAD).astype(jnp.float32)
    projected = jnp.einsum('thd,hdf->htf', split_rows, feat_weight.astype(jnp.float32), precision=lax.Precision.HIGHEST)
    return (jax.nn.elu(projected) + 1.0).astype(jnp.bfloat16)

def reference(queries, keys, values, feat_weight, norm_gain, counts, offsets):
    position = trace_positions(counts, offsets)
    packed_q = jnp.zeros(queries.shape, queries.dtype).at[position].set(queries)
    packed_k = jnp.zeros(keys.shape, keys.dtype).at[position].set(keys)
    packed_v = jnp.zeros(values.shape, values.dtype).at[position].set(values)
    inner = jnp.arange(TOK_DEV, dtype=jnp.int32)
    causal = inner[:, None] >= inner[None, :]
    gain = norm_gain.astype(jnp.float32).reshape(HEADS, 1, VDIM)

    def block_step(state, block):
        block_q, block_k, block_v = block
        phi_query = feature_map(block_q, feat_weight).astype(jnp.float32)
        phi_key = feature_map(block_k, feat_weight).astype(jnp.float32)
        value_heads = block_v.reshape(TOK_DEV, HEADS, VDIM).transpose(1, 0, 2).astype(jnp.float32)
        scores = jnp.einsum('hsf,htf->hst', phi_query, phi_key, precision=lax.Precision.HIGHEST)
        scores = jnp.where(causal[None, :, :], scores, 0.0)
        attended = jnp.einsum('hst,htv->hsv', scores, value_heads, precision=lax.Precision.HIGHEST)
        attended = attended + jnp.einsum('hsf,hfv->hsv', phi_query, state, precision=lax.Precision.HIGHEST)
        state = state + jnp.einsum('htf,htv->hfv', phi_key, value_heads, precision=lax.Precision.HIGHEST)
        centre = lax.optimization_barrier(jnp.mean(attended, axis=2, keepdims=True))
        centred = attended - centre
        spread_sq = lax.optimization_barrier(jnp.mean(centred * centred, axis=2, keepdims=True))
        normed = centred * lax.rsqrt(spread_sq + 1e-05) * gain
        return (state, normed.transpose(1, 0, 2).reshape(TOK_DEV, HEADS * VDIM).astype(jnp.bfloat16))
    blocks = (packed_q.reshape(N_SEQ, TOK_DEV, -1), packed_k.reshape(N_SEQ, TOK_DEV, -1), packed_v.reshape(N_SEQ, TOK_DEV, -1))
    initial = jnp.zeros((HEADS, FEAT, VDIM), jnp.float32)
    final_state, normed_blocks = lax.scan(block_step, initial, blocks)
    normed = normed_blocks.reshape(TOKENS, HEADS * VDIM)
    return normed[position]
```

```python
import functools

import jax
import jax.numpy as jnp
from jax import lax
from jax.experimental import pallas as pl
from jax.experimental.pallas import tpu as pltpu
from jax.sharding import PartitionSpec as P

MESH = pl.DeviceIdType.MESH
F32 = jnp.float32
BF16 = jnp.bfloat16
GROUPS = 4


def kernel(
    n,
    heads,
    q_ref,
    k_ref,
    v_ref,
    w_ref,
    gain_ref,
    counts_ref,
    offsets_ref,
    out_ref,
    q_buf,
    k_buf,
    v_buf,
    w_buf,
    gain_buf,
    counts_buf,
    offsets_buf,
    load_sem,
    kv_send,
    kv_recv,
    q_send,
    q_recv,
    phi_kt,
    phi_q,
    posr,
    post,
    posc,
    acc,
    wqa,
    wqb,
    wkt,
    out_send,
    out_recv,
    kv_send_sem,
    kv_recv_sem,
    q_send_sem,
    q_recv_sem,
    back_send_sem,
    back_recv_sem,
):
    rows = q_ref.shape[0]
    width = q_ref.shape[1] // heads
    group = n // heads
    part_rows = rows // group
    part_half = part_rows // 2
    me = lax.axis_index("seq")
    head = me // group
    part = me % group
    near = n // 2

    def partner(step):
        return jnp.bitwise_xor(me, step)

    loads = [
        pltpu.make_async_copy(src, dst, load_sem.at[i])
        for i, (src, dst) in enumerate(
            (
                (k_ref, k_buf),
                (v_ref, v_buf),
                (q_ref, q_buf),
                (counts_ref, counts_buf),
                (offsets_ref, offsets_buf),
                (w_ref.at[head], w_buf),
                (gain_ref, gain_buf),
            )
        )
    ]
    for load in loads:
        load.start()

    barrier = pltpu.get_barrier_semaphore()

    def greet(step, carry):
        pl.semaphore_signal(
            barrier, inc=1, device_id={"seq": partner(n - step)}, device_id_type=MESH
        )
        return carry

    lax.fori_loop(1, n, greet, 0)

    for load in loads[:3]:
        load.wait()

    for pair in range(heads // 2):
        lanes = slice(2 * width * pair, 2 * width * (pair + 1))
        k = k_buf[:, lanes]
        v = v_buf[:, lanes]
        kv_send[2 * pair] = jnp.concatenate([k[:, :width], v[:, :width]], axis=1)
        kv_send[2 * pair + 1] = jnp.concatenate([k[:, width:], v[:, width:]], axis=1)
        for piece in range(group):
            top = slice(piece * part_rows, piece * part_rows + part_half)
            low = slice(piece * part_rows + part_half, (piece + 1) * part_rows)
            a = q_buf[top, lanes]
            b = q_buf[low, lanes]
            q_send[2 * pair * group + piece] = jnp.concatenate([a[:, :width], b[:, :width]], axis=1)
            q_send[(2 * pair + 1) * group + piece] = jnp.concatenate(
                [a[:, width:], b[:, width:]], axis=1
            )

    pl.semaphore_wait(barrier, n - 1)

    def send_kv(step):
        peer = partner(step)
        return pltpu.make_async_remote_copy(
            src_ref=kv_send.at[peer // group],
            dst_ref=kv_recv.at[step],
            send_sem=kv_send_sem.at[step],
            recv_sem=kv_recv_sem.at[step],
            device_id={"seq": peer},
            device_id_type=MESH,
        )

    def send_q(step):
        peer = partner(step)
        return pltpu.make_async_remote_copy(
            src_ref=q_send.at[peer],
            dst_ref=q_recv.at[step],
            send_sem=q_send_sem.at[step],
            recv_sem=q_recv_sem.at[step],
            device_id={"seq": peer},
            device_id_type=MESH,
        )

    def back(step):
        return pltpu.make_async_remote_copy(
            src_ref=out_send.at[step],
            dst_ref=out_recv.at[step],
            send_sem=back_send_sem.at[step],
            recv_sem=back_recv_sem.at[step],
            device_id={"seq": partner(step)},
            device_id_type=MESH,
        )

    def start_near(step, carry):
        send_kv(step).start()
        send_q(step).start()
        return carry

    def start_kv(step, carry):
        send_kv(step).start()
        return carry

    def start_q(step, carry):
        send_q(step).start()
        return carry

    lax.fori_loop(1, near, start_near, 0)
    lax.fori_loop(near, n, start_kv, 0)
    lax.fori_loop(near, n, start_q, 0)
    kv_recv[0] = kv_send[head]
    q_recv[0] = q_send[me]

    for load in loads[3:]:
        load.wait()

    lane = lax.broadcasted_iota(jnp.int32, (n, rows), 1)
    start = jnp.zeros((n, 1), jnp.int32)
    position = lane
    for d in range(n):
        count = counts_buf[:, d : d + 1]
        inside = (lane >= start) & (lane < start + count)
        position = position + jnp.where(inside, d * rows + offsets_buf[:, d : d + 1] - start, 0)
        start = start + count
    position = position.astype(F32)
    posr[...] = position
    if n < rows:
        position = jnp.concatenate([position, jnp.zeros((rows - n, rows), F32)], axis=0)
    post[...] = position.T
    mine = post[pl.ds(pl.multiple_of(part * part_rows, part_rows), part_rows), :]
    for j in range(n):
        posc[j * part_rows : (j + 1) * part_rows, :] = jnp.broadcast_to(
            mine[:, j : j + 1], (part_rows, 128)
        )

    w = w_buf[...]
    blank = jnp.zeros_like(w)
    wqa[...] = jnp.concatenate([w, blank], axis=0)
    wqb[...] = jnp.concatenate([blank, w], axis=0)
    wkt[...] = wqa[...].astype(F32).T.astype(BF16)
    gain_row = gain_buf[...].astype(F32).reshape(1, -1)
    gain = jnp.zeros((1, width), F32)
    for h in range(heads):
        gain = gain + jnp.where(head == h, gain_row[:, h * width : (h + 1) * width], 0.0)

    def feature(z):
        return jnp.where(z > 0.0, z + 1.0, jnp.exp(jnp.minimum(z, 0.0))).astype(BF16)

    per = n // GROUPS
    tile_r = per * part_rows
    tile_s = per * rows

    def take_keys(g):
        x = kv_recv[g * per : (g + 1) * per].reshape(tile_s, 2 * width)
        keys = lax.dot_general(wkt[...], x, (((1,), (1,)), ((), ())), preferred_element_type=F32)
        phi_kt[:, g * tile_s : (g + 1) * tile_s] = feature(keys)

    def take_queries(first, count):
        x = q_recv[pl.ds(first, count)].reshape(count * part_half, 2 * width)
        top = jnp.dot(x, wqa[...], preferred_element_type=F32)
        low = jnp.dot(x, wqb[...], preferred_element_type=F32)
        return jnp.concatenate([feature(top), feature(low)], axis=0)

    def places(first, count):
        blocks = []
        for offset in (0, part_half):
            for i in range(count):
                at = partner(first + i) * part_rows + offset
                blocks.append(posc[pl.ds(pl.multiple_of(at, part_half), part_half), :])
        return jnp.concatenate(blocks, axis=0)

    def tile(phi, place, g):
        scores = jnp.dot(
            phi, phi_kt[:, g * tile_s : (g + 1) * tile_s], preferred_element_type=F32
        )
        later = jnp.concatenate([place] * per, axis=1)
        earlier = jnp.concatenate(
            [posr[pl.ds(partner(g * per + i), 1), :] for i in range(per)], axis=1
        )
        scores = jnp.where(earlier <= later, scores, 0.0)
        high = scores.astype(BF16)
        low = (scores - high.astype(F32)).astype(BF16)
        vals = kv_recv[g * per : (g + 1) * per].reshape(tile_s, 2 * width)
        return jnp.dot(high, vals, preferred_element_type=F32) + jnp.dot(
            low, vals, preferred_element_type=F32
        )

    def finish(first, count, attended):
        attended = attended[:, width:]
        centre = jnp.mean(attended, axis=1, keepdims=True)
        centred = attended - centre
        spread = jnp.mean(centred * centred, axis=1, keepdims=True)
        normed = (centred * lax.rsqrt(spread + 1e-05) * gain).astype(BF16)
        half = count * part_half
        packed = jnp.concatenate([normed[:half], normed[half:]], axis=1)
        out_send[pl.ds(first, count)] = packed.reshape(count, part_half, 2 * width)

    def rows_of(g):
        return slice(g * tile_r, (g + 1) * tile_r)

    nears = GROUPS // 2
    for g in range(GROUPS):
        for step in range(g * per, (g + 1) * per):
            if step > 0:
                send_kv(step).wait_recv()
                if g < nears:
                    send_q(step).wait_recv()
        take_keys(g)
        if g < nears:
            phi_q[rows_of(g), :] = take_queries(g * per, per)
            fresh = None
            for k in range(g + 1):
                more = tile(phi_q[rows_of(g), :], places(g * per, per), k)
                fresh = more if fresh is None else fresh + more
            acc[rows_of(g), :] = fresh
        for r in range(min(g, nears)):
            acc[rows_of(r), :] = acc[rows_of(r), :] + tile(
                phi_q[rows_of(r), :], places(r * per, per), g
            )
    for g in range(nears):
        finish(g * per, per, acc[rows_of(g), :])
        for step in range(g * per, (g + 1) * per):
            if step > 0:
                back(step).start()

    few = per // 2

    def late(piece, carry):
        first = near + piece * few
        for i in range(few):
            send_q(first + i).wait_recv()
        phi = take_queries(first, few)
        place = places(first, few)
        total = tile(phi, place, 0)
        for g in range(1, GROUPS):
            total = total + tile(phi, place, g)
        finish(first, few, total)
        for i in range(few):
            back(first + i).start()
        return carry

    lax.fori_loop(0, near // few, late, 0)
    out_recv[0] = out_send[0]

    def collect(step, carry):
        back(step).wait_recv()
        return carry

    lax.fori_loop(1, n, collect, 0)

    for piece in range(group):
        first = slice(piece * part_rows, piece * part_rows + part_half)
        second = slice(piece * part_rows + part_half, (piece + 1) * part_rows)
        for pair in range(heads // 2):
            lanes = slice(2 * width * pair, 2 * width * (pair + 1))
            a = out_recv[partner(2 * pair * group + piece)]
            b = out_recv[partner((2 * pair + 1) * group + piece)]
            out_ref[first, lanes] = jnp.concatenate([a[:, :width], b[:, :width]], axis=1)
            out_ref[second, lanes] = jnp.concatenate([a[:, width:], b[:, width:]], axis=1)

    def drain(step, carry):
        send_kv(step).wait_send()
        send_q(step).wait_send()
        back(step).wait_send()
        return carry

    lax.fori_loop(1, n, drain, 0)


def per_device(n, queries, keys, values, feat_weight, norm_gain, counts, offsets):
    rows = queries.shape[0]
    heads, width, feat = feat_weight.shape
    group = n // heads
    part_rows = rows // group
    total = n * rows
    lanes = 2 * width
    return pl.pallas_call(
        functools.partial(kernel, n, heads),
        out_shape=jax.ShapeDtypeStruct(queries.shape, BF16),
        in_specs=[pl.BlockSpec(memory_space=pltpu.HBM)] * 7,
        out_specs=pl.BlockSpec(memory_space=pltpu.VMEM),
        scratch_shapes=[
            pltpu.VMEM(queries.shape, BF16),
            pltpu.VMEM(keys.shape, BF16),
            pltpu.VMEM(values.shape, BF16),
            pltpu.VMEM((width, feat), BF16),
            pltpu.VMEM(norm_gain.shape, BF16),
            pltpu.VMEM(counts.shape, jnp.int32),
            pltpu.VMEM(offsets.shape, jnp.int32),
            pltpu.SemaphoreType.DMA((7,)),
            pltpu.VMEM((heads, rows, lanes), BF16),
            pltpu.VMEM((n, rows, lanes), BF16),
            pltpu.VMEM((n, part_rows // 2, lanes), BF16),
            pltpu.VMEM((n, part_rows // 2, lanes), BF16),
            pltpu.VMEM((feat, total), BF16),
            pltpu.VMEM((n * part_rows // 2, feat), BF16),
            pltpu.VMEM((n, rows), F32),
            pltpu.VMEM((rows, max(n, rows)), F32),
            pltpu.VMEM((n * part_rows, 128), F32),
            pltpu.VMEM((n * part_rows // 2, lanes), F32),
            pltpu.VMEM((lanes, feat), BF16),
            pltpu.VMEM((lanes, feat), BF16),
            pltpu.VMEM((feat, lanes), BF16),
            pltpu.VMEM((n, part_rows // 2, lanes), BF16),
            pltpu.VMEM((n, part_rows // 2, lanes), BF16),
            pltpu.SemaphoreType.DMA((n,)),
            pltpu.SemaphoreType.DMA((n,)),
            pltpu.SemaphoreType.DMA((n,)),
            pltpu.SemaphoreType.DMA((n,)),
            pltpu.SemaphoreType.DMA((n,)),
            pltpu.SemaphoreType.DMA((n,)),
        ],
        compiler_params=pltpu.CompilerParams(
            collective_id=0, has_side_effects=True, vmem_limit_bytes=67043328
        ),
    )(queries, keys, values, feat_weight, norm_gain, counts, offsets)


def solution(mesh):
    in_specs = (
        P(("dp", "seq"), None),
        P(("dp", "seq"), None),
        P(("dp", "seq"), None),
        P(),
        P(),
        P("dp", None),
        P("dp", None),
    )
    return jax.shard_map(
        functools.partial(per_device, mesh.shape["seq"]),
        mesh=mesh,
        in_specs=in_specs,
        out_specs=P(("dp", "seq"), None),
        check_vma=False,
    )
```
